256 devices in a mesh: gx: 32 (over x, y, z_hi), gy: 8 (over z_lo, core).
Axes of the slice: x: 4, y: 4, z: 8 (z_hi: 2, z_lo: 4; z = z_hi * 4 + z_lo), core: 2. Of those that a mesh axis runs over, the one named last changes fastest.
Arguments:
- noisy: bfloat16 [2, 2048, 2048], P(None, 'gx', 'gy'), may hold values from -6 to 6
- dilations: int32 [3], replicated, may hold values from 1 to 256, as said below
- conv_weights: float32 [3, 4, 27], replicated, may hold values from -0.625 to 0.625
- biases: float32 [3], replicated, may hold values from -3 to 3
- mix_weights: float32 [4], replicated, may hold values from -3 to 3
Outputs:
- denoised: bfloat16 [2, 2048, 2048], P(None, 'gx', 'gy')
The draws below stay inside these ranges and needn't reach their ends.
Inputs may be any that keep to these rules, and one draw needn't show every extreme that they name: `dilations`: every layer's dilation lies in 1 .. 256; some layer has dilation 256.
All inputs are finite; a program needn't handle non-finite values.
Results may differ from the reference program's by a relative error of at most 0.0065.
Values sent between devices are 32-bit elements; how exact they have to be, the bound alone decides.
A program may use at most 64 MiB of HBM per device.

```python
import jax
import jax.numpy as jnp
from jax import lax

Z = 2
LAYERS = 3
DMAX = 256
NX = 2048
NY = 2048


def draw_dilations(key, part):
    first_key = jax.random.fold_in(key, 11)
    second_key = jax.random.fold_in(key, 23)
    values = jax.random.randint(first_key, (LAYERS,), 1, DMAX + 1)
    chosen = jax.random.randint(second_key, (), 0, LAYERS)
    return jnp.where(jnp.arange(LAYERS) == chosen, DMAX, values).astype(jnp.int32)


def level_of(stream_key, dims, pieces, smallest, high):
    def one(dim, parts):
        steps = jax.random.uniform(jax.random.fold_in(jax.random.fold_in(stream_key, 6), dim), (parts,), jnp.float32, smallest / len(pieces), high / len(pieces))
        return jnp.repeat(jnp.exp(steps), dims[dim] // parts).reshape((-1,) + (1,) * (len(dims) - dim - 1))

    factor_of = one(*pieces[0])
    for cut in pieces[1:]:
        factor_of = factor_of * one(*cut)
    return factor_of


def gaussian(own_key, dims, width, most, split=(), dtype=jnp.bfloat16):
    entries = jax.random.normal(own_key, dims, jnp.float32) * width
    if len(split) > 0:
        entries = level_of(own_key, dims, split, -0.22, 0.18) * entries
    return jnp.clip(entries, min=-most, max=most).astype(dtype)


def setup_inputs(seed: int = 0) -> dict:
    key_list = jax.random.split(jax.random.key(seed), 6)
    return {
        "noisy": gaussian(key_list[0], (Z, NX, NY), 1.0, 6.0, ((1, 32), (2, 8))),
        "dilations": draw_dilations(jax.random.fold_in(key_list[5], 71), 0),
        "conv_weights": gaussian(key_list[2], (LAYERS, LAYERS + 1, 27), (27 * LAYERS) ** -0.5, 0.625, (), jnp.float32),
        "biases": gaussian(key_list[3], (LAYERS,), 0.5, 3.0, (), jnp.float32),
        "mix_weights": gaussian(key_list[4], (LAYERS + 1,), (LAYERS + 1) ** -0.5, 3.0, (), jnp.float32),
    }


def shift_along(source_field, axis_index, offset):
    widths = [(0, 0)] * source_field.ndim
    widths[axis_index] = (DMAX, DMAX)
    padded = jnp.pad(source_field, widths)
    start_index = (offset + DMAX).astype(jnp.int32)
    return lax.dynamic_slice_in_dim(padded, start_index, source_field.shape[axis_index], axis_index)


def tap_sums(feature_maps, layer_weights):
    map_count = len(feature_maps)
    stacked = jnp.stack(feature_maps).astype(jnp.float32)
    padded = jnp.pad(stacked, ((0, 0), (1, 1), (0, 0), (0, 0)))
    depth = stacked.shape[1]
    zstack = jnp.stack([padded[:, shift_index:shift_index + depth] for shift_index in range(3)])
    kernel = layer_weights[:map_count].reshape(map_count, 3, 3, 3)
    return jnp.einsum("cjzxy,jcab->abzxy", zstack, kernel, precision=lax.Precision.HIGHEST,
                      preferred_element_type=jnp.float32)


def reference(noisy, dilations, conv_weights, biases, mix_weights):
    feature_maps = [noisy]
    for layer_index in range(LAYERS):
        reach = dilations[layer_index]
        partial_value = tap_sums(feature_maps, conv_weights[layer_index])
        summed = jnp.zeros(noisy.shape, jnp.float32)
        for row_tap in range(3):
            for col_tap in range(3):
                shifted = shift_along(partial_value[row_tap, col_tap], 1, (row_tap - 1) * reach)
                shifted = shift_along(shifted, 2, (col_tap - 1) * reach)
                summed = summed + shifted
        feature_maps.append(jax.nn.relu(summed + biases[layer_index]).astype(jnp.bfloat16))
    output = jnp.zeros(noisy.shape, jnp.float32)
    for map_index in range(LAYERS + 1):
        output = output + mix_weights[map_index] * feature_maps[map_index].astype(jnp.float32)
    return output.astype(jnp.bfloat16)
```

```python
import functools
import itertools

import jax
import jax.numpy as jnp
from jax import lax
from jax.experimental import pallas as pl
from jax.experimental.pallas import tpu as pltpu
from jax.sharding import PartitionSpec as P

LAYERS = 3
LANES = 128
CHUNKS = 1

NEAR, FAR, FULL = 0, 1, 2
TILES = {NEAR: (0, 1, 2), FAR: (2, 3, 4), FULL: (4,)}
SEND_ORDER = {NEAR: (1, 2), FAR: (3, 4, 2), FULL: (4,)}
COMBOS = [c for c in itertools.product((NEAR, FAR, FULL), repeat=LAYERS) if FULL in c]


def kernel(classes, shape, gx_count, gy_count, noisy_ref, dil_ref, w_ref, bias_ref, mix_ref, out_ref, *scratch):
    depth, width, height = shape
    blocks = height // LANES
    rows = width // CHUNKS
    scratch = list(scratch)
    ext = [[scratch.pop(0) for _ in range(CHUNKS)] for _ in range(LAYERS)]
    centre = [scratch.pop(0) for _ in range(LAYERS)]
    above = [scratch.pop(0) for _ in range(LAYERS)]
    below = [scratch.pop(0) for _ in range(LAYERS)]
    sends = [
        (above[i], below[i]) if classes[i] == NEAR else (scratch.pop(0), scratch.pop(0)) for i in range(LAYERS)
    ]
    y_send, y_recv, x_send, x_recv = scratch
    gx, gy = lax.axis_index("gx"), lax.axis_index("gy")

    def exists(dx, dy):
        return (gx + dx >= 0) & (gx + dx < gx_count) & (gy + dy >= 0) & (gy + dy < gy_count)

    offsets = sorted({t for c in classes for t in TILES[c] if t > 0})
    partners = [(s * t, 0) for t in offsets for s in (1, -1)] + [(0, 1), (0, -1)]
    barrier = pltpu.get_barrier_semaphore()
    expected = jnp.int32(0)
    for dx, dy in partners:

        @pl.when(exists(dx, dy))
        def _():
            pl.semaphore_signal(barrier, inc=1, device_id={"gx": gx + dx, "gy": gy + dy})

        expected = expected + exists(dx, dy).astype(jnp.int32)

    for chunk in range(CHUNKS):
        part = pl.ds(chunk * rows, rows)
        for k in range(blocks):
            ext[0][chunk][blocks + k] = noisy_ref[:, part, k * LANES : (k + 1) * LANES].astype(jnp.float32)

    @pl.when(gy == 0)
    def _():
        for i in range(LAYERS):
            for chunk in range(CHUNKS):
                ext[i][chunk][0:blocks] = jnp.zeros((blocks, depth, rows, LANES), jnp.float32)

    @pl.when(gy == gy_count - 1)
    def _():
        for i in range(LAYERS):
            for chunk in range(CHUNKS):
                ext[i][chunk][2 * blocks : 3 * blocks] = jnp.zeros((blocks, depth, rows, LANES), jnp.float32)

    for i in range(LAYERS):
        tiles = TILES[classes[i]]
        for slot, t in enumerate(tiles):
            if t == 0:
                continue
            up = pl.ds(slot * width, width)
            down = pl.ds((len(tiles) - 1 - slot) * width, width)

            @pl.when(gx + t >= gx_count)
            def _():
                above[i][:, :, up] = jnp.zeros((blocks, depth, width, LANES), jnp.float32)

            @pl.when(gx - t < 0)
            def _():
                below[i][:, :, down] = jnp.zeros((blocks, depth, width, LANES), jnp.float32)

    pl.semaphore_wait(barrier, expected)

    def y_copy(i, chunk, side):
        own = ext[i][chunk].at[pl.ds(blocks, blocks)]
        there = ext[i][chunk].at[pl.ds(0 if side == 1 else 2 * blocks, blocks)]
        index = (i * CHUNKS + chunk) * 2 + (0 if side == 1 else 1)
        return pltpu.make_async_remote_copy(
            src_ref=own,
            dst_ref=there,
            send_sem=y_send.at[index],
            recv_sem=y_recv.at[index],
            device_id={"gx": gx, "gy": gy + side},
        )

    def x_copy(i, chunk, t, sign):
        tiles = TILES[classes[i]]
        slot = tiles.index(t)
        place = slot if sign == 1 else len(tiles) - 1 - slot
        source = sends[i][0] if sign == 1 else sends[i][1]
        base = (0 if sign == 1 else (len(tiles) - 1) * width) if classes[i] == NEAR else 0
        target = above[i] if sign == 1 else below[i]
        index = ((i * CHUNKS + chunk) * 3 + slot) * 2 + (0 if sign == 1 else 1)
        return pltpu.make_async_remote_copy(
            src_ref=source.at[:, :, pl.ds(base + chunk * rows, rows)],
            dst_ref=target.at[:, :, pl.ds(place * width + chunk * rows, rows)],
            send_sem=x_send.at[index],
            recv_sem=x_recv.at[index],
            device_id={"gx": gx - sign * t, "gy": gy},
        )

    def start_y(i, chunk):
        for side in (1, -1):

            @pl.when(exists(0, side))
            def _():
                y_copy(i, chunk, side).start()

    for chunk in range(CHUNKS):
        start_y(0, chunk)

    for i in range(LAYERS):
        reach = jnp.clip(dil_ref[i], 1, blocks * LANES)
        plus = reach + blocks * LANES
        minus = blocks * LANES - reach
        plus_tile, plus_lane = plus // LANES, plus % LANES
        minus_tile, minus_lane = minus // LANES, minus % LANES
        lane = lax.broadcasted_iota(jnp.int32, (rows, LANES), 1)

        for chunk in range(CHUNKS):
            for side in (1, -1):

                @pl.when(exists(0, -side))
                def _():
                    y_copy(i, chunk, side).wait_recv()

            up_base = chunk * rows
            down_base = chunk * rows + ((len(TILES[classes[i]]) - 1) * width if classes[i] == NEAR else 0)

            def sums(k, _):
                def shifted(j, z, tile, amount):
                    first = ext[j][chunk][tile + k, z]
                    second = ext[j][chunk][jnp.minimum(tile + k + 1, 3 * blocks - 1), z]
                    turn = lax.rem(LANES - amount, LANES)
                    first = pltpu.roll(first, turn, 1)
                    second = pltpu.roll(second, turn, 1)
                    return jnp.where(lane < LANES - amount, first, second)

                totals = [[None] * depth for _ in range(3)]
                for j in range(i + 1):
                    for z_in in range(depth):
                        values = (
                            shifted(j, z_in, minus_tile, minus_lane),
                            ext[j][chunk][blocks + k, z_in],
                            shifted(j, z_in, plus_tile, plus_lane),
                        )
                        for b in range(3):
                            for z_out in range(depth):
                                c = z_in - z_out + 1
                                if c < 0 or c > 2:
                                    continue
                                for a in range(3):
                                    term = w_ref[i, j, 9 * c + 3 * a + b] * values[b]
                                    old = totals[a][z_out]
                                    totals[a][z_out] = term if old is None else old + term
                for z_out in range(depth):
                    centre[i][k, z_out, pl.ds(chunk * rows, rows)] = totals[1][z_out]
                    sends[i][0][k, z_out, pl.ds(up_base, rows)] = totals[2][z_out]
                    sends[i][1][k, z_out, pl.ds(down_base, rows)] = totals[0][z_out]
                return 0

            lax.fori_loop(0, blocks, sums, 0)
            for t in SEND_ORDER[classes[i]]:
                for sign in (1, -1):

                    @pl.when(exists(-sign * t, 0))
                    def _():
                        x_copy(i, chunk, t, sign).start()

        for t in SEND_ORDER[classes[i]]:
            for chunk in range(CHUNKS):
                for sign in (1, -1):

                    @pl.when(exists(sign * t, 0))
                    def _():
                        x_copy(i, chunk, t, sign).wait_recv()

        if classes[i] == NEAR:
            up_start, down_start = reach, 2 * width - reach
        elif classes[i] == FAR:
            up_start, down_start = reach - 2 * width, 4 * width - reach
        else:
            up_start, down_start = 0, 0
        if classes[i] != FULL:
            up_start = jnp.clip(up_start, 0, 2 * width)
            down_start = jnp.clip(down_start, 0, 2 * width)

        for chunk in range(CHUNKS):
            for z in range(depth):
                for k in range(blocks):
                    value = centre[i][k, z, pl.ds(chunk * rows, rows)]
                    value = value + above[i][k, z, pl.ds(up_start + chunk * rows, rows)]
                    value = value + below[i][k, z, pl.ds(down_start + chunk * rows, rows)]
                    value = jnp.maximum(value + bias_ref[i], 0.0).astype(jnp.bfloat16).astype(jnp.float32)
                    if i < LAYERS - 1:
                        ext[i + 1][chunk][blocks + k, z] = value
                    else:
                        mixed = mix_ref[0] * ext[0][chunk][blocks + k, z]
                        for j in range(1, LAYERS):
                            mixed = mixed + mix_ref[j] * ext[j][chunk][blocks + k, z]
                        mixed = mixed + mix_ref[LAYERS] * value
                        out_ref[z, pl.ds(chunk * rows, rows), k * LANES : (k + 1) * LANES] = mixed.astype(jnp.bfloat16)
            if i < LAYERS - 1:
                start_y(i + 1, chunk)

    for i in range(LAYERS):
        for chunk in range(CHUNKS):
            for side in (1, -1):

                @pl.when(exists(0, side))
                def _():
                    y_copy(i, chunk, side).wait_send()

            for t in SEND_ORDER[classes[i]]:
                for sign in (1, -1):

                    @pl.when(exists(-sign * t, 0))
                    def _():
                        x_copy(i, chunk, t, sign).wait_send()


def run(number, gx_count, gy_count, noisy, dilations, conv_weights, biases, mix_weights):
    classes = COMBOS[number]
    depth, width, height = noisy.shape
    blocks = height // LANES
    rows = width // CHUNKS
    scratch = [pltpu.VMEM((3 * blocks, depth, rows, LANES), jnp.float32)] * (LAYERS * CHUNKS)
    scratch += [pltpu.VMEM((blocks, depth, width, LANES), jnp.float32)] * LAYERS
    for _ in range(2):
        scratch += [pltpu.VMEM((blocks, depth, len(TILES[c]) * width, LANES), jnp.float32) for c in classes]
    for c in classes:
        if c != NEAR:
            scratch += [pltpu.VMEM((blocks, depth, width, LANES), jnp.float32)] * 2
    y_count, x_count = LAYERS * CHUNKS * 2, LAYERS * CHUNKS * 3 * 2
    scratch += [pltpu.SemaphoreType.DMA((y_count,))] * 2 + [pltpu.SemaphoreType.DMA((x_count,))] * 2
    smem = pl.BlockSpec(memory_space=pltpu.SMEM)
    vmem = pl.BlockSpec(memory_space=pltpu.VMEM)
    return pl.pallas_call(
        functools.partial(kernel, classes, noisy.shape, gx_count, gy_count),
        out_shape=jax.ShapeDtypeStruct(noisy.shape, jnp.bfloat16),
        in_specs=[vmem, smem, smem, smem, smem],
        out_specs=vmem,
        scratch_shapes=scratch,
        compiler_params=pltpu.CompilerParams(collective_id=number, has_side_effects=True),
        name="msd_" + "".join(str(c) for c in classes),
    )(noisy, dilations, conv_weights, biases, mix_weights)


def body(gx_count, gy_count, noisy, dilations, conv_weights, biases, mix_weights):
    width = noisy.shape[1]
    kinds = jnp.where(dilations >= 4 * width, FULL, jnp.where(dilations >= 2 * width, FAR, NEAR))
    code = kinds[0] * 9 + kinds[1] * 3 + kinds[2]
    numbers = [0] * 27
    for number, c in enumerate(COMBOS):
        numbers[c[0] * 9 + c[1] * 3 + c[2]] = number
    number = jnp.sum(jnp.where(jnp.arange(27) == code, jnp.array(numbers), 0))
    branches = [functools.partial(run, n, gx_count, gy_count) for n in range(len(COMBOS))]
    return lax.switch(number, branches, noisy, dilations, conv_weights, biases, mix_weights)


def solution(mesh):
    return jax.shard_map(
        functools.partial(body, mesh.shape["gx"], mesh.shape["gy"]),
        mesh=mesh,
        in_specs=(P(None, "gx", "gy"), P(), P(), P(), P()),
        out_specs=P(None, "gx", "gy"),
        check_vma=False,
    )
```

```python
import functools
import itertools

import jax
import jax.numpy as jnp
from jax import lax
from jax.experimental import pallas as pl
from jax.experimental.pallas import tpu as pltpu
from jax.sharding import PartitionSpec as P

LAYERS = 3
LANES = 128
CHUNKS = 4

NEAR, FAR, FULL = 0, 1, 2
TILES = {NEAR: (0, 1, 2), FAR: (2, 3, 4), FULL: (4,)}
SEND_ORDER = {NEAR: (1, 2), FAR: (3, 4, 2), FULL: (4,)}
COMBOS = [c for c in itertools.product((NEAR, FAR, FULL), repeat=LAYERS) if FULL in c]


def kernel(classes, shape, gx_count, gy_count, noisy_ref, dil_ref, w_ref, bias_ref, mix_ref, out_ref, ext, *scratch):
    depth, width, height = shape
    blocks = height // LANES
    rows = width // CHUNKS
    scratch = list(scratch)
    centre = scratch.pop(0)
    above = [scratch.pop(0) for _ in range(LAYERS)]
    below = [scratch.pop(0) for _ in range(LAYERS)]
    sends = [
        (above[i], below[i]) if classes[i] == NEAR else (scratch.pop(0), scratch.pop(0)) for i in range(LAYERS)
    ]
    y_send, y_recv, x_send, x_recv = scratch
    gx, gy = lax.axis_index("gx"), lax.axis_index("gy")

    def exists(dx, dy):
        if dy == 0:
            return (gx + dx < gx_count) if dx > 0 else (gx + dx >= 0)
        return (gy + dy < gy_count) if dy > 0 else (gy + dy >= 0)

    offsets = sorted({t for c in classes for t in TILES[c] if t > 0})
    partners = [(s * t, 0) for t in offsets for s in (1, -1)] + [(0, 1), (0, -1)]
    barrier = pltpu.get_barrier_semaphore()
    expected = jnp.int32(0)
    for dx, dy in partners:

        @pl.when(exists(dx, dy))
        def _():
            pl.semaphore_signal(barrier, inc=1, device_id={"gx": gx + dx, "gy": gy + dy})

        expected = expected + exists(dx, dy).astype(jnp.int32)

    for k in range(blocks):
        for chunk in range(CHUNKS):
            piece = noisy_ref[:, chunk * rows : (chunk + 1) * rows, k * LANES : (k + 1) * LANES]
            ext[0, chunk, blocks + k] = piece.astype(jnp.float32)

    def clear_y(first):
        def step(n, _):
            zero = jnp.zeros((blocks, depth, rows, LANES), jnp.float32)
            ext[n // CHUNKS, n % CHUNKS, pl.ds(first, blocks)] = zero
            return 0

        lax.fori_loop(0, LAYERS * CHUNKS, step, 0)

    pl.when(gy == 0)(lambda: clear_y(0))
    pl.when(gy == gy_count - 1)(lambda: clear_y(2 * blocks))

    def clear_x(ref, place):
        def step(n, _):
            ref[n // depth, n % depth, pl.ds(place * width, width)] = jnp.zeros((width, LANES), jnp.float32)
            return 0

        lax.fori_loop(0, blocks * depth, step, 0)

    for i in range(LAYERS):
        tiles = TILES[classes[i]]
        for slot, t in enumerate(tiles):
            if t > 0:
                pl.when(gx + t >= gx_count)(functools.partial(clear_x, above[i], slot))
                pl.when(gx - t < 0)(functools.partial(clear_x, below[i], len(tiles) - 1 - slot))

    pl.semaphore_wait(barrier, expected)

    def y_copy(i, chunk, side, count=1):
        index = 0 if side == 1 else 1
        chunks = pl.ds(chunk, count)
        return pltpu.make_async_remote_copy(
            src_ref=ext.at[i, chunks, pl.ds(blocks, blocks)],
            dst_ref=ext.at[i, chunks, pl.ds(0 if side == 1 else 2 * blocks, blocks)],
            send_sem=y_send.at[i, index],
            recv_sem=y_recv.at[i, index, chunk],
            device_id={"gx": gx, "gy": gy + side},
        )

    def x_copy(i, t, sign, start, count):
        tiles = TILES[classes[i]]
        slot = tiles.index(t)
        place = slot if sign == 1 else len(tiles) - 1 - slot
        source = sends[i][0] if sign == 1 else sends[i][1]
        base = (0 if sign == 1 else (len(tiles) - 1) * width) if classes[i] == NEAR else 0
        target = above[i] if sign == 1 else below[i]
        index = (i * 3 + slot) * 2 + (0 if sign == 1 else 1)
        return pltpu.make_async_remote_copy(
            src_ref=source.at[:, :, pl.ds(base + start, count)],
            dst_ref=target.at[:, :, pl.ds(place * width + start, count)],
            send_sem=x_send.at[index],
            recv_sem=x_recv.at[index],
            device_id={"gx": gx - sign * t, "gy": gy},
        )

    def start_y(i, chunk):
        for side in (1, -1):
            pl.when(exists(0, side))(lambda: y_copy(i, chunk, side).start())

    def first(chunk, _):
        start_y(0, chunk)
        return 0

    lax.fori_loop(0, CHUNKS, first, 0)
    lane = lax.broadcasted_iota(jnp.int32, (rows, LANES), 1)

    for i in range(LAYERS):
        full = classes[i] == FULL
        reach = jnp.clip(dil_ref[i], 1, blocks * LANES)
        plus_tile, plus_lane = reach // LANES, reach % LANES
        minus_tile, minus_lane = (blocks * LANES - reach) // LANES, (blocks * LANES - reach) % LANES
        up_base = 0
        down_base = (len(TILES[classes[i]]) - 1) * width if classes[i] == NEAR else 0

        def shifted(tiles, choices, tile, amount):
            picked = []
            for k in range(blocks + 1):
                value = tiles[min(k + choices - 1, len(tiles) - 1)]
                for n in range(choices - 2, -1, -1):
                    value = jnp.where(tile == n, tiles[min(k + n, len(tiles) - 1)], value)
                picked.append(pltpu.roll(value, lax.rem(LANES - amount, LANES), 1))
            inside = lane < LANES - amount
            return [jnp.where(inside, picked[k], picked[k + 1]) for k in range(blocks)]

        def sums(chunk, _):
            for side in (1, -1):
                pl.when(exists(0, -side))(lambda: y_copy(i, chunk, side).wait_recv())

            def add_map(j, totals):
                totals = list(totals)
                for z_in in range(depth):
                    tiles = [ext[j, chunk, n, z_in] for n in range(3 * blocks)]
                    own = tiles[blocks : 2 * blocks]
                    if full:
                        values = (tiles[:blocks], own, tiles[2 * blocks :])
                    else:
                        values = (
                            shifted(tiles[: 2 * blocks], blocks, minus_tile, minus_lane),
                            own,
                            shifted(tiles[blocks:], blocks + 1, plus_tile, plus_lane),
                        )
                    for b in range(3):
                        for z_out in range(depth):
                            c = z_in - z_out + 1
                            if c < 0 or c > 2:
                                continue
                            for a in range(3):
                                weight = w_ref[i, j, 9 * c + 3 * a + b]
                                for k in range(blocks):
                                    n = (a * depth + z_out) * blocks + k
                                    totals[n] = totals[n] + weight * values[b][k]
                return tuple(totals)

            totals = (jnp.zeros((rows, LANES), jnp.float32),) * (3 * depth * blocks)
            totals = lax.fori_loop(0, i + 1, add_map, totals)
            start = pl.multiple_of(chunk * rows, rows)
            for z in range(depth):
                for k in range(blocks):
                    sends[i][0][k, z, pl.ds(up_base + start, rows)] = totals[(2 * depth + z) * blocks + k]
                    sends[i][1][k, z, pl.ds(down_base + start, rows)] = totals[z * blocks + k]
                    centre[k, z, pl.ds(start, rows)] = totals[(depth + z) * blocks + k]
            for t in SEND_ORDER[classes[i]]:
                for sign in (1, -1):
                    pl.when(exists(-sign * t, 0))(lambda: x_copy(i, t, sign, start, rows).start())
            return 0

        lax.fori_loop(0, CHUNKS, sums, 0)

        for t in SEND_ORDER[classes[i]]:
            for sign in (1, -1):
                pl.when(exists(sign * t, 0))(lambda: x_copy(i, t, sign, 0, width).wait_recv())

        if classes[i] == NEAR:
            up_start = jnp.clip(reach, 0, 2 * width)
            down_start = jnp.clip(2 * width - reach, 0, 2 * width)
        elif classes[i] == FAR:
            up_start = jnp.clip(reach - 2 * width, 0, 2 * width)
            down_start = jnp.clip(4 * width - reach, 0, 2 * width)
        else:
            up_start, down_start = 0, 0

        def combine(chunk, _):
            start = pl.multiple_of(chunk * rows, rows)
            for z in range(depth):
                for k in range(blocks):
                    value = centre[k, z, pl.ds(start, rows)]
                    value = value + above[i][k, z, pl.ds(up_start + start, rows)]
                    value = value + below[i][k, z, pl.ds(down_start + start, rows)]
                    value = jnp.maximum(value + bias_ref[i], 0.0).astype(jnp.bfloat16).astype(jnp.float32)
                    if i < LAYERS - 1:
                        ext[i + 1, chunk, blocks + k, z] = value
                    else:
                        mixed = mix_ref[0] * ext[0, chunk, blocks + k, z]
                        for j in range(1, LAYERS):
                            mixed = mixed + mix_ref[j] * ext[j, chunk, blocks + k, z]
                        mixed = mixed + mix_ref[LAYERS] * value
                        out_ref[z, pl.ds(start, rows), k * LANES : (k + 1) * LANES] = mixed.astype(jnp.bfloat16)
            if i < LAYERS - 1:
                start_y(i + 1, chunk)
            return 0

        lax.fori_loop(0, CHUNKS, combine, 0)

    for i in range(LAYERS):
        for side in (1, -1):
            pl.when(exists(0, side))(lambda: y_copy(i, 0, side, CHUNKS).wait_send())
        for t in SEND_ORDER[classes[i]]:
            for sign in (1, -1):
                pl.when(exists(-sign * t, 0))(lambda: x_copy(i, t, sign, 0, width).wait_send())


def run(number, gx_count, gy_count, noisy, dilations, conv_weights, biases, mix_weights):
    classes = COMBOS[number]
    depth, width, height = noisy.shape
    blocks = height // LANES
    rows = width // CHUNKS
    scratch = [pltpu.VMEM((LAYERS, CHUNKS, 3 * blocks, depth, rows, LANES), jnp.float32)]
    scratch += [pltpu.VMEM((blocks, depth, width, LANES), jnp.float32)]
    for _ in range(2):
        scratch += [pltpu.VMEM((blocks, depth, len(TILES[c]) * width, LANES), jnp.float32) for c in classes]
    for c in classes:
        if c != NEAR:
            scratch += [pltpu.VMEM((blocks, depth, width, LANES), jnp.float32)] * 2
    scratch += [pltpu.SemaphoreType.DMA((LAYERS, 2)), pltpu.SemaphoreType.DMA((LAYERS, 2, CHUNKS))]
    scratch += [pltpu.SemaphoreType.DMA((LAYERS * 6,))] * 2
    smem = pl.BlockSpec(memory_space=pltpu.SMEM)
    vmem = pl.BlockSpec(memory_space=pltpu.VMEM)
    return pl.pallas_call(
        functools.partial(kernel, classes, noisy.shape, gx_count, gy_count),
        out_shape=jax.ShapeDtypeStruct(noisy.shape, jnp.bfloat16),
        in_specs=[vmem, smem, smem, smem, smem],
        out_specs=vmem,
        scratch_shapes=scratch,
        compiler_params=pltpu.CompilerParams(collective_id=number, has_side_effects=True),
        name="msd_" + "".join(str(c) for c in classes),
    )(noisy, dilations, conv_weights, biases, mix_weights)


def body(gx_count, gy_count, noisy, dilations, conv_weights, biases, mix_weights):
    width = noisy.shape[1]
    place = lax.iota(jnp.int32, LAYERS)
    power = jnp.where(place == 0, 9, jnp.where(place == 1, 3, 1))
    kinds = (dilations >= 2 * width).astype(jnp.int32) + (dilations >= 4 * width).astype(jnp.int32)
    code = jnp.sum(kinds * power)
    branches = [lambda noisy, *_: jnp.zeros_like(noisy)] * (FULL * 13 + 1)
    for number, classes in enumerate(COMBOS):
        place = 9 * classes[0] + 3 * classes[1] + classes[2]
        branches[place] = functools.partial(run, number, gx_count, gy_count)
    return lax.switch(code, branches, noisy, dilations, conv_weights, biases, mix_weights)


def solution(mesh):
    return jax.shard_map(
        functools.partial(body, mesh.shape["gx"], mesh.shape["gy"]),
        mesh=mesh,
        in_specs=(P(None, "gx", "gy"), P(), P(), P(), P()),
        out_specs=P(None, "gx", "gy"),
        check_vma=False,
    )
```

```python
import functools
import itertools

import jax
import jax.numpy as jnp
from jax import lax
from jax.experimental import pallas as pl
from jax.experimental.pallas import tpu as pltpu
from jax.sharding import PartitionSpec as P

LAYERS = 3
LANES = 128
CHUNKS = 4
SKEW = 2

NEAR, FAR, FULL = 0, 1, 2
TILES = {NEAR: (0, 1, 2), FAR: (2, 3, 4), FULL: (4,)}
SEND_ORDER = {NEAR: (1, 2), FAR: (3, 4, 2), FULL: (4,)}
COMBOS = [c for c in itertools.product((NEAR, FAR, FULL), repeat=LAYERS) if FULL in c]


BOTH, SENDER, RECEIVER = 0, 1, 2


def modes_of(classes):
    modes = []
    for i, c in enumerate(classes):
        if c == FULL:
            modes.append(BOTH)
        elif i == 0 or (i == 1 and classes[0] != FAR):
            modes.append(SENDER)
        else:
            modes.append(RECEIVER)
    return modes


def plan(classes):
    modes = modes_of(classes)
    remote = [[t for t in TILES[c] if t > 0] for c in classes]
    counts = [len(r) * 2 * (1 if m == RECEIVER else CHUNKS) for r, m in zip(remote, modes)]
    return modes, remote, counts


def kernel(classes, shape, gx_count, gy_count, *refs):
    given, out_ref, ext = refs[:5], refs[5], refs[6]
    held, fetch_sem, scratch = refs[7:12], refs[12], refs[13:]
    noisy_ref, dil_ref, w_ref, bias_ref, mix_ref = held
    fetches = [pltpu.make_async_copy(given[n], held[n], fetch_sem.at[n]) for n in range(5)]
    for fetch in fetches:
        fetch.start()

    depth, width, height = shape
    blocks = height // LANES
    rows = width // CHUNKS
    modes, remote, counts = plan(classes)
    scratch = list(scratch)
    centre = [scratch.pop(0), scratch.pop(0)]
    above, below, sends, natural = [], [], [], []
    for i in range(LAYERS):
        above.append(scratch.pop(0))
        below.append(scratch.pop(0))
        own = classes[i] == NEAR and modes[i] == RECEIVER
        sends.append((above[i], below[i]) if own else (scratch.pop(0), scratch.pop(0)))
        natural.append((scratch.pop(0), scratch.pop(0)) if modes[i] == SENDER else None)
    y_send, y_recv, x_send, x_recv = scratch
    gx, gy = lax.axis_index("gx"), lax.axis_index("gy")

    def exists(dx, dy):
        if dy == 0:
            return (gx + dx < gx_count) if dx > 0 else (gx + dx >= 0)
        return (gy + dy < gy_count) if dy > 0 else (gy + dy >= 0)

    offsets = sorted({t for r in remote for t in r})
    partners = [(s * t, 0) for t in offsets for s in (1, -1)] + [(0, 1), (0, -1)]
    barrier = pltpu.get_barrier_semaphore()
    expected = jnp.int32(0)
    for dx, dy in partners:

        @pl.when(exists(dx, dy))
        def _():
            pl.semaphore_signal(barrier, inc=1, device_id={"gx": gx + dx, "gy": gy + dy})

        expected = expected + exists(dx, dy).astype(jnp.int32)

    for fetch in fetches:
        fetch.wait()
    for k in range(blocks):
        for chunk in range(CHUNKS):
            piece = noisy_ref[:, chunk * rows : (chunk + 1) * rows, k * LANES : (k + 1) * LANES]
            ext[0, chunk, blocks + k] = piece.astype(jnp.float32)

    def clear_y(first):
        def step(n, _):
            zero = jnp.zeros((blocks, depth, rows, LANES), jnp.float32)
            ext[n // CHUNKS, n % CHUNKS, pl.ds(first, blocks)] = zero
            return 0

        lax.fori_loop(0, LAYERS * CHUNKS, step, 0)

    pl.when(gy == 0)(lambda: clear_y(0))
    pl.when(gy == gy_count - 1)(lambda: clear_y(2 * blocks))

    def clear_x(ref, place):
        def step(n, _):
            ref[n // depth, n % depth, pl.ds(place * width, width)] = jnp.zeros((width, LANES), jnp.float32)
            return 0

        lax.fori_loop(0, blocks * depth, step, 0)

    def place_of(i, t, sign):
        tiles = TILES[classes[i]] if modes[i] == RECEIVER else remote[i]
        slot = tiles.index(t)
        return len(tiles) - 1 - slot if sign == -1 and modes[i] == RECEIVER else slot

    for i in range(LAYERS):
        for t in remote[i]:
            pl.when(gx + t >= gx_count)(functools.partial(clear_x, above[i], place_of(i, t, 1)))
            pl.when(gx - t < 0)(functools.partial(clear_x, below[i], place_of(i, t, -1)))

    pl.semaphore_wait(barrier, expected)

    def y_copy(i, chunk, side, count=1):
        index = 0 if side == 1 else 1
        chunks = pl.ds(chunk, count)
        return pltpu.make_async_remote_copy(
            src_ref=ext.at[i, chunks, pl.ds(blocks, blocks)],
            dst_ref=ext.at[i, chunks, pl.ds(0 if side == 1 else 2 * blocks, blocks)],
            send_sem=y_send.at[i, index],
            recv_sem=y_recv.at[i, index, chunk],
            device_id={"gx": gx, "gy": gy + side},
        )

    def bases(i):
        if classes[i] == NEAR and modes[i] == RECEIVER:
            return 0, (len(TILES[NEAR]) - 1) * width
        return 0, 0

    def x_copy(i, t, sign, chunk, count=1):
        way = 0 if sign == 1 else 1
        target = (above[i], below[i])[way]
        index = remote[i].index(t) * 2 + way
        arrival = index if modes[i] == RECEIVER else index * CHUNKS + chunk
        start, size = chunk * rows, count * rows
        return pltpu.make_async_remote_copy(
            src_ref=sends[i][way].at[:, :, pl.ds(bases(i)[way] + start, size)],
            dst_ref=target.at[:, :, pl.ds(place_of(i, t, sign) * width + start, size)],
            send_sem=x_send.at[sum(len(r) * 2 for r in remote[:i]) + index],
            recv_sem=x_recv.at[sum(counts[:i]) + arrival],
            device_id={"gx": gx - sign * t, "gy": gy},
        )

    def start_y(i, chunk):
        for side in (1, -1):
            pl.when(exists(0, side))(lambda: y_copy(i, chunk, side).start())

    def start_x(i, chunk):
        for t in SEND_ORDER[classes[i]]:
            for sign in (1, -1):
                pl.when(exists(-sign * t, 0))(lambda: x_copy(i, t, sign, chunk).start())

    def wait_x(i, chunk, count=1):
        for t in SEND_ORDER[classes[i]]:
            for sign in (1, -1):
                pl.when(exists(sign * t, 0))(lambda: x_copy(i, t, sign, chunk, count).wait_recv())

    lane = lax.broadcasted_iota(jnp.int32, (rows, LANES), 1)
    line = lax.broadcasted_iota(jnp.int32, (rows, LANES), 0)
    reaches = [jnp.clip(dil_ref[i], 1, blocks * LANES) for i in range(LAYERS)]

    def sums(i, chunk):
        reach = reaches[i]
        plus_tile, plus_lane = reach // LANES, reach % LANES
        minus_tile, minus_lane = (blocks * LANES - reach) // LANES, (blocks * LANES - reach) % LANES

        def shifted(tiles, choices, tile, amount):
            picked = []
            for k in range(blocks + 1):
                value = tiles[min(k + choices - 1, len(tiles) - 1)]
                for n in range(choices - 2, -1, -1):
                    value = jnp.where(tile == n, tiles[min(k + n, len(tiles) - 1)], value)
                picked.append(pltpu.roll(value, lax.rem(LANES - amount, LANES), 1))
            inside = lane < LANES - amount
            return [jnp.where(inside, picked[k], picked[k + 1]) for k in range(blocks)]

        for side in (1, -1):
            pl.when(exists(0, -side))(lambda: y_copy(i, chunk, side).wait_recv())

        def add_map(j, totals):
            totals = list(totals)
            for z_in in range(depth):
                tiles = [ext[j, chunk, n, z_in] for n in range(3 * blocks)]
                own = tiles[blocks : 2 * blocks]
                if classes[i] == FULL:
                    values = (tiles[:blocks], own, tiles[2 * blocks :])
                else:
                    values = (
                        shifted(tiles[: 2 * blocks], blocks, minus_tile, minus_lane),
                        own,
                        shifted(tiles[blocks:], blocks + 1, plus_tile, plus_lane),
                    )
                for b in range(3):
                    for z_out in range(depth):
                        c = z_in - z_out + 1
                        if c < 0 or c > 2:
                            continue
                        for a in range(3):
                            weight = w_ref[i, j, 9 * c + 3 * a + b]
                            for k in range(blocks):
                                n = (a * depth + z_out) * blocks + k
                                totals[n] = totals[n] + weight * values[b][k]
            return tuple(totals)

        totals = (jnp.zeros((rows, LANES), jnp.float32),) * (3 * depth * blocks)
        totals = lax.fori_loop(0, i + 1, add_map, totals)
        start = chunk * rows
        for z in range(depth):
            for k in range(blocks):
                up, down = totals[(2 * depth + z) * blocks + k], totals[z * blocks + k]
                if modes[i] == SENDER:
                    for half in (0, width):
                        natural[i][0][k, z, pl.ds(start + half, rows)] = up
                        natural[i][1][k, z, pl.ds(start + half, rows)] = down
                else:
                    sends[i][0][k, z, pl.ds(bases(i)[0] + start, rows)] = up
                    sends[i][1][k, z, pl.ds(bases(i)[1] + start, rows)] = down
                centre[i % 2][k, z, pl.ds(start, rows)] = totals[(depth + z) * blocks + k]
        if modes[i] != SENDER:
            start_x(i, chunk)

    def pack(i, chunk):
        turn = reaches[i] % width
        for way, first in ((0, turn), (1, width - turn)):
            for z in range(depth):
                for k in range(blocks):
                    piece = natural[i][way][k, z, pl.ds(first + chunk * rows, rows)]
                    sends[i][way][k, z, pl.ds(chunk * rows, rows)] = piece
        start_x(i, chunk)

    def arrived(i, chunk):
        reach = reaches[i]
        start = chunk * rows
        if modes[i] == RECEIVER:
            least = TILES[classes[i]][0] * width
            up_start = jnp.clip(reach - least, 0, 2 * width)
            down_start = jnp.clip(2 * width + least - reach, 0, 2 * width)
            return (
                lambda k, z: above[i][k, z, pl.ds(up_start + start, rows)],
                lambda k, z: below[i][k, z, pl.ds(down_start + start, rows)],
            )
        if modes[i] == BOTH:
            return (
                lambda k, z: above[i][k, z, pl.ds(start, rows)],
                lambda k, z: below[i][k, z, pl.ds(start, rows)],
            )
        turn = reach % width
        low = reach // width == TILES[classes[i]][0]

        def choose(way, inside, k, z):
            parts = []
            for t in TILES[classes[i]]:
                if t == 0:
                    parts.append(sends[i][way][k, z, pl.ds(start, rows)])
                else:
                    place = place_of(i, t, 1) * width
                    parts.append((above[i], below[i])[way][k, z, pl.ds(place + start, rows)])
            near = jnp.where(low, parts[0], parts[1])
            far = jnp.where(low, parts[1], parts[2])
            return jnp.where(inside, near, far)

        return (
            lambda k, z: choose(0, line + start + turn < width, k, z),
            lambda k, z: choose(1, line + start >= turn, k, z),
        )

    def combine(i, chunk):
        start = chunk * rows
        up, down = arrived(i, chunk)
        for z in range(depth):
            for k in range(blocks):
                value = centre[i % 2][k, z, pl.ds(start, rows)] + up(k, z) + down(k, z)
                value = jnp.maximum(value + bias_ref[i], 0.0).astype(jnp.bfloat16).astype(jnp.float32)
                if i < LAYERS - 1:
                    ext[i + 1, chunk, blocks + k, z] = value
                else:
                    mixed = mix_ref[0] * ext[0, chunk, blocks + k, z]
                    for j in range(1, LAYERS):
                        mixed = mixed + mix_ref[j] * ext[j, chunk, blocks + k, z]
                    mixed = mixed + mix_ref[LAYERS] * value
                    out_ref[z, pl.ds(start, rows), k * LANES : (k + 1) * LANES] = mixed.astype(jnp.bfloat16)
        if i < LAYERS - 1:
            start_y(i + 1, chunk)

    def loop(count, *steps):
        def step(n, _):
            for one in steps:
                one(n)
            return 0

        lax.fori_loop(0, count, step, 0)

    loop(CHUNKS, lambda chunk: start_y(0, chunk))
    for i in range(LAYERS):
        joined = i > 0 and modes[i - 1] != RECEIVER and modes[i] != SENDER
        if not joined:
            if i > 0:
                if modes[i - 1] == RECEIVER:
                    wait_x(i - 1, 0, CHUNKS)
                    loop(CHUNKS, functools.partial(combine, i - 1))
                else:
                    loop(CHUNKS, functools.partial(wait_x, i - 1), functools.partial(combine, i - 1))
            loop(CHUNKS, functools.partial(sums, i))
            if modes[i] == SENDER:
                loop(CHUNKS, functools.partial(pack, i))
        else:

            def next_sums(n):
                pl.when(n >= SKEW)(lambda: sums(i, n - SKEW))

            def last_combine(n):
                @pl.when(n < CHUNKS)
                def _():
                    wait_x(i - 1, n)
                    combine(i - 1, n)

            loop(CHUNKS + SKEW, next_sums, last_combine)
    if modes[LAYERS - 1] == RECEIVER:
        wait_x(LAYERS - 1, 0, CHUNKS)
        loop(CHUNKS, functools.partial(combine, LAYERS - 1))
    else:
        loop(CHUNKS, functools.partial(wait_x, LAYERS - 1), functools.partial(combine, LAYERS - 1))

    for i in range(LAYERS):
        for side in (1, -1):
            pl.when(exists(0, side))(lambda: y_copy(i, 0, side, CHUNKS).wait_send())
        for t in SEND_ORDER[classes[i]]:
            for sign in (1, -1):
                pl.when(exists(-sign * t, 0))(lambda: x_copy(i, t, sign, 0, CHUNKS).wait_send())


def run(number, gx_count, gy_count, noisy, dilations, conv_weights, biases, mix_weights):
    classes = COMBOS[number]
    modes, remote, counts = plan(classes)
    depth, width, height = noisy.shape
    blocks = height // LANES
    rows = width // CHUNKS
    scratch = [pltpu.VMEM((LAYERS, CHUNKS, 3 * blocks, depth, rows, LANES), jnp.float32)]
    scratch += [pltpu.VMEM(noisy.shape, noisy.dtype)]
    scratch += [pltpu.SMEM(x.shape, x.dtype) for x in (dilations, conv_weights, biases, mix_weights)]
    scratch += [pltpu.SemaphoreType.DMA((5,))]

    def tiles(count):
        return [pltpu.VMEM((blocks, depth, count * width, LANES), jnp.float32)] * 2

    scratch += tiles(1)
    for i in range(LAYERS):
        scratch += tiles(len(TILES[classes[i]] if modes[i] == RECEIVER else remote[i]))
        if classes[i] != NEAR or modes[i] != RECEIVER:
            scratch += tiles(1)
        if modes[i] == SENDER:
            scratch += tiles(2)
    scratch += [pltpu.SemaphoreType.DMA((LAYERS, 2)), pltpu.SemaphoreType.DMA((LAYERS, 2, CHUNKS))]
    scratch += [pltpu.SemaphoreType.DMA((sum(len(r) * 2 for r in remote),)), pltpu.SemaphoreType.DMA((sum(counts),))]
    return pl.pallas_call(
        functools.partial(kernel, classes, noisy.shape, gx_count, gy_count),
        out_shape=jax.ShapeDtypeStruct(noisy.shape, jnp.bfloat16),
        in_specs=[pl.BlockSpec(memory_space=pltpu.HBM)] * 5,
        out_specs=pl.BlockSpec(memory_space=pltpu.VMEM),
        scratch_shapes=scratch,
        compiler_params=pltpu.CompilerParams(collective_id=number, has_side_effects=True),
        name="msd_" + "".join(str(c) for c in classes),
    )(*(pltpu.with_memory_space_constraint(x, pltpu.HBM) for x in (noisy, dilations, conv_weights, biases, mix_weights)))


def body(gx_count, gy_count, noisy, dilations, conv_weights, biases, mix_weights):
    width = noisy.shape[1]
    place = lax.iota(jnp.int32, LAYERS)
    power = jnp.where(place == 0, 9, jnp.where(place == 1, 3, 1))
    kinds = (dilations >= 2 * width).astype(jnp.int32) + (dilations >= 4 * width).astype(jnp.int32)
    code = jnp.sum(kinds * power)
    branches = [lambda noisy, *_: jnp.zeros_like(noisy)] * (FULL * 13 + 1)
    for number, classes in enumerate(COMBOS):
        place = 9 * classes[0] + 3 * classes[1] + classes[2]
        branches[place] = functools.partial(run, number, gx_count, gy_count)
    return lax.switch(code, branches, noisy, dilations, conv_weights, biases, mix_weights)


def solution(mesh):
    return jax.shard_map(
        functools.partial(body, mesh.shape["gx"], mesh.shape["gy"]),
        mesh=mesh,
        in_specs=(P(None, "gx", "gy"), P(), P(), P(), P()),
        out_specs=P(None, "gx", "gy"),
        check_vma=False,
    )
```

```python
import functools
import itertools

import jax
import jax.numpy as jnp
from jax import lax
from jax.experimental import pallas as pl
from jax.experimental.pallas import tpu as pltpu
from jax.sharding import PartitionSpec as P

LAYERS = 3
LANES = 128
CHUNKS = 4
SKEW = 2

NEAR, FAR, FULL, HALF = 0, 1, 2, 3
TILES = {NEAR: (0, 1, 2), FAR: (2, 3, 4), FULL: (4,), HALF: (0, 1, 2)}
SEND_ORDER = {NEAR: (1, 2), FAR: (3, 4, 2), FULL: (4,), HALF: (1, 2)}
COMBOS = [c for c in itertools.product(range(4), range(4), range(3)) if FULL in c]


BOTH, SENDER, RECEIVER = 0, 1, 2


def modes_of(classes):
    modes = []
    for i, c in enumerate(classes):
        if c == FULL:
            modes.append(BOTH)
        elif c == HALF or i == 0 or (i == 1 and classes[0] != FAR):
            modes.append(SENDER)
        else:
            modes.append(RECEIVER)
    return modes


def plan(classes):
    modes = modes_of(classes)
    remote = [[t for t in TILES[c] if t > 0] for c in classes]
    counts = [len(r) * 2 * (1 if m == RECEIVER else CHUNKS) for r, m in zip(remote, modes)]
    return modes, remote, counts


def kernel(classes, shape, gx_count, gy_count, *refs):
    given, out_ref, ext = refs[:5], refs[5], refs[6]
    held, fetch_sem, scratch = refs[7:12], refs[12], refs[13:]
    noisy_ref, dil_ref, w_ref, bias_ref, mix_ref = held
    fetches = [pltpu.make_async_copy(given[n], held[n], fetch_sem.at[n]) for n in range(5)]
    for fetch in fetches:
        fetch.start()

    depth, width, height = shape
    blocks = height // LANES
    rows = width // CHUNKS
    modes, remote, counts = plan(classes)
    scratch = list(scratch)
    centre = [scratch.pop(0), scratch.pop(0)]
    above, below, sends, natural, halves = [], [], [], [], []
    for i in range(LAYERS):
        above.append(scratch.pop(0))
        below.append(scratch.pop(0))
        own = classes[i] == NEAR and modes[i] == RECEIVER
        sends.append((above[i], below[i]) if own else (scratch.pop(0), scratch.pop(0)))
        natural.append((scratch.pop(0), scratch.pop(0)) if modes[i] == SENDER else None)
        halves.append((scratch.pop(0), scratch.pop(0)) if classes[i] == HALF else None)
    y_send, y_recv, x_send, x_recv = scratch
    gx, gy = lax.axis_index("gx"), lax.axis_index("gy")

    def exists(dx, dy):
        if dy == 0:
            return (gx + dx < gx_count) if dx > 0 else (gx + dx >= 0)
        return (gy + dy < gy_count) if dy > 0 else (gy + dy >= 0)

    offsets = sorted({t for r in remote for t in r})
    partners = [(s * t, 0) for t in offsets for s in (1, -1)] + [(0, 1), (0, -1)]
    barrier = pltpu.get_barrier_semaphore()
    expected = jnp.int32(0)
    for dx, dy in partners:

        @pl.when(exists(dx, dy))
        def _():
            pl.semaphore_signal(barrier, inc=1, device_id={"gx": gx + dx, "gy": gy + dy})

        expected = expected + exists(dx, dy).astype(jnp.int32)

    for fetch in fetches:
        fetch.wait()
    for k in range(blocks):
        for chunk in range(CHUNKS):
            piece = noisy_ref[:, chunk * rows : (chunk + 1) * rows, k * LANES : (k + 1) * LANES]
            ext[0, chunk, blocks + k] = piece.astype(jnp.float32)

    def clear_y(first):
        def step(n, _):
            zero = jnp.zeros((blocks, depth, rows, LANES), jnp.float32)
            ext[n // CHUNKS, n % CHUNKS, pl.ds(first, blocks)] = zero
            return 0

        lax.fori_loop(0, LAYERS * CHUNKS, step, 0)

    pl.when(gy == 0)(lambda: clear_y(0))
    pl.when(gy == gy_count - 1)(lambda: clear_y(2 * blocks))

    def clear_x(ref, place):
        def step(n, _):
            ref[n // depth, n % depth, pl.ds(place * width, width)] = jnp.zeros((width, LANES), jnp.float32)
            return 0

        lax.fori_loop(0, blocks * depth, step, 0)

    def place_of(i, t, sign):
        tiles = TILES[classes[i]] if modes[i] == RECEIVER else remote[i]
        slot = tiles.index(t)
        return len(tiles) - 1 - slot if sign == -1 and modes[i] == RECEIVER else slot

    for i in range(LAYERS):
        for t in remote[i]:
            pl.when(gx + t >= gx_count)(functools.partial(clear_x, above[i], place_of(i, t, 1)))
            pl.when(gx - t < 0)(functools.partial(clear_x, below[i], place_of(i, t, -1)))

    pl.semaphore_wait(barrier, expected)

    def y_copy(i, chunk, side, count=1):
        index = 0 if side == 1 else 1
        chunks = pl.ds(chunk, count)
        return pltpu.make_async_remote_copy(
            src_ref=ext.at[i, chunks, pl.ds(blocks, blocks)],
            dst_ref=ext.at[i, chunks, pl.ds(0 if side == 1 else 2 * blocks, blocks)],
            send_sem=y_send.at[i, index],
            recv_sem=y_recv.at[i, index, chunk],
            device_id={"gx": gx, "gy": gy + side},
        )

    def bases(i):
        if classes[i] == NEAR and modes[i] == RECEIVER:
            return 0, (len(TILES[NEAR]) - 1) * width
        return 0, 0

    def x_copy(i, t, sign, chunk, count=1):
        way = 0 if sign == 1 else 1
        target = (above[i], below[i])[way]
        index = remote[i].index(t) * 2 + way
        arrival = index if modes[i] == RECEIVER else index * CHUNKS + chunk
        start, size = chunk * rows, count * rows
        source = (halves[i] if is_half(i, t) else sends[i])[way]
        return pltpu.make_async_remote_copy(
            src_ref=source.at[:, :, pl.ds(bases(i)[way] + start, size)],
            dst_ref=target.at[:, :, pl.ds(place_of(i, t, sign) * width + start, size)],
            send_sem=x_send.at[sum(len(r) * 2 for r in remote[:i]) + index],
            recv_sem=x_recv.at[sum(counts[:i]) + arrival],
            device_id={"gx": gx - sign * t, "gy": gy},
        )

    def start_y(i, chunk):
        for side in (1, -1):
            pl.when(exists(0, side))(lambda: y_copy(i, chunk, side).start())

    def is_half(i, t):
        return classes[i] == HALF and t == 1

    def used(i, t, chunk):
        return (chunk < CHUNKS // 2) if is_half(i, t) else True

    def start_x(i, chunk):
        for t in SEND_ORDER[classes[i]]:
            for sign in (1, -1):
                pl.when(exists(-sign * t, 0) & used(i, t, chunk))(lambda: x_copy(i, t, sign, chunk).start())

    def wait_x(i, chunk, count=1):
        for t in SEND_ORDER[classes[i]]:
            for sign in (1, -1):
                pl.when(exists(sign * t, 0) & used(i, t, chunk))(lambda: x_copy(i, t, sign, chunk, count).wait_recv())

    lane = lax.broadcasted_iota(jnp.int32, (rows, LANES), 1)
    line = lax.broadcasted_iota(jnp.int32, (rows, LANES), 0)
    reaches = [jnp.clip(dil_ref[i], 1, blocks * LANES) for i in range(LAYERS)]

    def sums(i, chunk):
        reach = reaches[i]
        plus_tile, plus_lane = reach // LANES, reach % LANES
        minus_tile, minus_lane = (blocks * LANES - reach) // LANES, (blocks * LANES - reach) % LANES

        def shifted(tiles, choices, tile, amount):
            picked = []
            for k in range(blocks + 1):
                value = tiles[min(k + choices - 1, len(tiles) - 1)]
                for n in range(choices - 2, -1, -1):
                    value = jnp.where(tile == n, tiles[min(k + n, len(tiles) - 1)], value)
                picked.append(pltpu.roll(value, lax.rem(LANES - amount, LANES), 1))
            inside = lane < LANES - amount
            return [jnp.where(inside, picked[k], picked[k + 1]) for k in range(blocks)]

        for side in (1, -1):
            pl.when(exists(0, -side))(lambda: y_copy(i, chunk, side).wait_recv())

        def add_map(j, totals):
            totals = list(totals)
            for z_in in range(depth):
                tiles = [ext[j, chunk, n, z_in] for n in range(3 * blocks)]
                own = tiles[blocks : 2 * blocks]
                if classes[i] == FULL:
                    values = (tiles[:blocks], own, tiles[2 * blocks :])
                else:
                    values = (
                        shifted(tiles[: 2 * blocks], blocks, minus_tile, minus_lane),
                        own,
                        shifted(tiles[blocks:], blocks + 1, plus_tile, plus_lane),
                    )
                for b in range(3):
                    for z_out in range(depth):
                        c = z_in - z_out + 1
                        if c < 0 or c > 2:
                            continue
                        for a in range(3):
                            weight = w_ref[i, j, 9 * c + 3 * a + b]
                            for k in range(blocks):
                                n = (a * depth + z_out) * blocks + k
                                totals[n] = totals[n] + weight * values[b][k]
            return tuple(totals)

        totals = (jnp.zeros((rows, LANES), jnp.float32),) * (3 * depth * blocks)
        totals = lax.fori_loop(0, i + 1, add_map, totals)
        start = chunk * rows
        for z in range(depth):
            for k in range(blocks):
                up, down = totals[(2 * depth + z) * blocks + k], totals[z * blocks + k]
                if modes[i] == SENDER:
                    for half in (0, width):
                        natural[i][0][k, z, pl.ds(start + half, rows)] = up
                        natural[i][1][k, z, pl.ds(start + half, rows)] = down
                else:
                    sends[i][0][k, z, pl.ds(bases(i)[0] + start, rows)] = up
                    sends[i][1][k, z, pl.ds(bases(i)[1] + start, rows)] = down
                centre[i % 2][k, z, pl.ds(start, rows)] = totals[(depth + z) * blocks + k]
        if modes[i] != SENDER:
            start_x(i, chunk)

    def pack(i, chunk):
        turn = reaches[i] % width
        for way, first in ((0, turn), (1, width - turn)):
            for z in range(depth):
                for k in range(blocks):
                    piece = natural[i][way][k, z, pl.ds(first + chunk * rows, rows)]
                    sends[i][way][k, z, pl.ds(chunk * rows, rows)] = piece
        if classes[i] == HALF:
            low = reaches[i] < width

            @pl.when(chunk < CHUNKS // 2)
            def _():
                for way, first in ((0, turn), (1, width - turn)):
                    other = width // 2
                    skip = jnp.where(low, other, 0) if way == 0 else jnp.where(low, 0, other)
                    for z in range(depth):
                        for k in range(blocks):
                            piece = natural[i][way][k, z, pl.ds(first + skip + chunk * rows, rows)]
                            halves[i][way][k, z, pl.ds(chunk * rows, rows)] = piece

        start_x(i, chunk)

    def arrived(i, chunk):
        reach = reaches[i]
        start = chunk * rows
        if modes[i] == RECEIVER:
            least = TILES[classes[i]][0] * width
            up_start = jnp.clip(reach - least, 0, 2 * width)
            down_start = jnp.clip(2 * width + least - reach, 0, 2 * width)
            return (
                lambda k, z: above[i][k, z, pl.ds(up_start + start, rows)],
                lambda k, z: below[i][k, z, pl.ds(down_start + start, rows)],
            )
        if modes[i] == BOTH:
            return (
                lambda k, z: above[i][k, z, pl.ds(start, rows)],
                lambda k, z: below[i][k, z, pl.ds(start, rows)],
            )
        turn = reach % width
        low = reach // width == TILES[classes[i]][0]

        def choose(way, inside, k, z):
            parts = []
            for t in TILES[classes[i]]:
                if t == 0:
                    parts.append(sends[i][way][k, z, pl.ds(start, rows)])
                else:
                    place = place_of(i, t, 1) * width
                    at = lax.rem(chunk, CHUNKS // 2) * rows if is_half(i, t) else start
                    parts.append((above[i], below[i])[way][k, z, pl.ds(place + at, rows)])
            near = jnp.where(low, parts[0], parts[1])
            far = jnp.where(low, parts[1], parts[2])
            return jnp.where(inside, near, far)

        return (
            lambda k, z: choose(0, line + start + turn < width, k, z),
            lambda k, z: choose(1, line + start >= turn, k, z),
        )

    def combine(i, chunk):
        start = chunk * rows
        up, down = arrived(i, chunk)
        for z in range(depth):
            for k in range(blocks):
                value = centre[i % 2][k, z, pl.ds(start, rows)] + up(k, z) + down(k, z)
                value = jnp.maximum(value + bias_ref[i], 0.0).astype(jnp.bfloat16).astype(jnp.float32)
                if i < LAYERS - 1:
                    ext[i + 1, chunk, blocks + k, z] = value
                else:
                    mixed = mix_ref[0] * ext[0, chunk, blocks + k, z]
                    for j in range(1, LAYERS):
                        mixed = mixed + mix_ref[j] * ext[j, chunk, blocks + k, z]
                    mixed = mixed + mix_ref[LAYERS] * value
                    out_ref[z, pl.ds(start, rows), k * LANES : (k + 1) * LANES] = mixed.astype(jnp.bfloat16)
        if i < LAYERS - 1:
            start_y(i + 1, chunk)

    def loop(count, *steps):
        def step(n, _):
            for one in steps:
                one(n)
            return 0

        lax.fori_loop(0, count, step, 0)

    loop(CHUNKS, lambda chunk: start_y(0, chunk))
    for i in range(LAYERS):
        joined = i > 0 and modes[i - 1] != RECEIVER and modes[i] != SENDER
        if not joined:
            if i > 0:
                if modes[i - 1] == RECEIVER:
                    wait_x(i - 1, 0, CHUNKS)
                    loop(CHUNKS, functools.partial(combine, i - 1))
                else:
                    loop(CHUNKS, functools.partial(wait_x, i - 1), functools.partial(combine, i - 1))
            loop(CHUNKS, functools.partial(sums, i))
            if modes[i] == SENDER:
                loop(CHUNKS, functools.partial(pack, i))
        else:

            def next_sums(n):
                pl.when(n >= SKEW)(lambda: sums(i, n - SKEW))

            def last_combine(n):
                @pl.when(n < CHUNKS)
                def _():
                    wait_x(i - 1, n)
                    combine(i - 1, n)

            loop(CHUNKS + SKEW, next_sums, last_combine)
    if modes[LAYERS - 1] == RECEIVER:
        wait_x(LAYERS - 1, 0, CHUNKS)
        loop(CHUNKS, functools.partial(combine, LAYERS - 1))
    else:
        loop(CHUNKS, functools.partial(wait_x, LAYERS - 1), functools.partial(combine, LAYERS - 1))

    for i in range(LAYERS):
        for side in (1, -1):
            pl.when(exists(0, side))(lambda: y_copy(i, 0, side, CHUNKS).wait_send())
        for t in SEND_ORDER[classes[i]]:
            for sign in (1, -1):
                count = CHUNKS // 2 if is_half(i, t) else CHUNKS
                pl.when(exists(-sign * t, 0))(lambda: x_copy(i, t, sign, 0, count).wait_send())


def run(number, gx_count, gy_count, noisy, dilations, conv_weights, biases, mix_weights):
    classes = COMBOS[number]
    modes, remote, counts = plan(classes)
    depth, width, height = noisy.shape
    blocks = height // LANES
    rows = width // CHUNKS
    scratch = [pltpu.VMEM((LAYERS, CHUNKS, 3 * blocks, depth, rows, LANES), jnp.float32)]
    scratch += [pltpu.VMEM(noisy.shape, noisy.dtype)]
    scratch += [pltpu.SMEM(x.shape, x.dtype) for x in (dilations, conv_weights, biases, mix_weights)]
    scratch += [pltpu.SemaphoreType.DMA((5,))]

    def tiles(count):
        return [pltpu.VMEM((blocks, depth, count * width, LANES), jnp.float32)] * 2

    scratch += tiles(1)
    for i in range(LAYERS):
        scratch += tiles(len(TILES[classes[i]] if modes[i] == RECEIVER else remote[i]))
        if classes[i] != NEAR or modes[i] != RECEIVER:
            scratch += tiles(1)
        if modes[i] == SENDER:
            scratch += tiles(2)
        if classes[i] == HALF:
            scratch += tiles(1)
    scratch += [pltpu.SemaphoreType.DMA((LAYERS, 2)), pltpu.SemaphoreType.DMA((LAYERS, 2, CHUNKS))]
    scratch += [pltpu.SemaphoreType.DMA((sum(len(r) * 2 for r in remote),)), pltpu.SemaphoreType.DMA((sum(counts),))]
    return pl.pallas_call(
        functools.partial(kernel, classes, noisy.shape, gx_count, gy_count),
        out_shape=jax.ShapeDtypeStruct(noisy.shape, jnp.bfloat16),
        in_specs=[pl.BlockSpec(memory_space=pltpu.HBM)] * 5,
        out_specs=pl.BlockSpec(memory_space=pltpu.VMEM),
        scratch_shapes=scratch,
        compiler_params=pltpu.CompilerParams(collective_id=number, has_side_effects=True),
        name="msd_" + "".join(str(c) for c in classes),
    )(*(pltpu.with_memory_space_constraint(x, pltpu.HBM) for x in (noisy, dilations, conv_weights, biases, mix_weights)))


def body(gx_count, gy_count, noisy, dilations, conv_weights, biases, mix_weights):
    width = noisy.shape[1]
    place = lax.iota(jnp.int32, LAYERS)
    power = jnp.where(place == 0, 12, jnp.where(place == 1, 3, 1))
    small = (dilations <= width // 2) | ((dilations >= 3 * width // 2) & (dilations < 2 * width))
    kinds = (dilations >= 2 * width).astype(jnp.int32) + (dilations >= 4 * width).astype(jnp.int32)
    kinds = jnp.where(small & (place < LAYERS - 1), HALF, kinds)
    code = jnp.sum(kinds * power)
    branches = [lambda noisy, *_: jnp.zeros_like(noisy)] * 48
    for number, classes in enumerate(COMBOS):
        place = 12 * classes[0] + 3 * classes[1] + classes[2]
        branches[place] = functools.partial(run, number, gx_count, gy_count)
    return lax.switch(code, branches, noisy, dilations, conv_weights, biases, mix_weights)


def solution(mesh):
    return jax.shard_map(
        functools.partial(body, mesh.shape["gx"], mesh.shape["gy"]),
        mesh=mesh,
        in_specs=(P(None, "gx", "gy"), P(), P(), P(), P()),
        out_specs=P(None, "gx", "gy"),
        check_vma=False,
    )
```

```python
import functools
import itertools

import jax
import jax.numpy as jnp
from jax import lax
from jax.experimental import pallas as pl
from jax.experimental.pallas import tpu as pltpu
from jax.sharding import PartitionSpec as P

LAYERS = 3
LANES = 128
CHUNKS = 8
SKEW = 4

NEAR, FAR, FULL, HALF = 0, 1, 2, 3
TILES = {NEAR: (0, 1, 2), FAR: (2, 3, 4), FULL: (4,), HALF: (0, 1, 2)}
SEND_ORDER = {NEAR: (1, 2), FAR: (3, 4, 2), FULL: (4,), HALF: (1, 2)}
COMBOS = [c for c in itertools.product(range(4), range(4), range(3)) if FULL in c]


BOTH, SENDER, RECEIVER = 0, 1, 2


def modes_of(classes):
    modes = []
    for i, c in enumerate(classes):
        if c == FULL:
            modes.append(BOTH)
        elif c == HALF or i == 0 or (i == 1 and classes[0] != FAR):
            modes.append(SENDER)
        else:
            modes.append(RECEIVER)
    return modes


def plan(classes):
    modes = modes_of(classes)
    remote = [[t for t in TILES[c] if t > 0] for c in classes]
    counts = [len(r) * 2 * (1 if m == RECEIVER else CHUNKS) for r, m in zip(remote, modes)]
    return modes, remote, counts


def kernel(classes, shape, gx_count, gy_count, *refs):
    given, out_ref, ext = refs[:5], refs[5], refs[6]
    held, fetch_sem, scratch = refs[7:12], refs[12], refs[13:]
    noisy_ref, dil_ref, w_ref, bias_ref, mix_ref = held
    fetches = [pltpu.make_async_copy(given[n], held[n], fetch_sem.at[n]) for n in range(5)]
    for fetch in fetches:
        fetch.start()

    depth, width, height = shape
    blocks = height // LANES
    rows = width // CHUNKS
    modes, remote, counts = plan(classes)
    scratch = list(scratch)
    centre = [scratch.pop(0), scratch.pop(0)]
    above, below, sends, natural, halves = [], [], [], [], []
    for i in range(LAYERS):
        above.append(scratch.pop(0))
        below.append(scratch.pop(0))
        own = classes[i] == NEAR and modes[i] == RECEIVER
        sends.append((above[i], below[i]) if own else (scratch.pop(0), scratch.pop(0)))
        natural.append((scratch.pop(0), scratch.pop(0)) if modes[i] == SENDER else None)
        halves.append((scratch.pop(0), scratch.pop(0)) if classes[i] == HALF else None)
    y_send, y_recv, x_send, x_recv = scratch
    gx, gy = lax.axis_index("gx"), lax.axis_index("gy")

    def exists(dx, dy):
        if dy == 0:
            return (gx + dx < gx_count) if dx > 0 else (gx + dx >= 0)
        return (gy + dy < gy_count) if dy > 0 else (gy + dy >= 0)

    offsets = sorted({t for r in remote for t in r})
    partners = [(s * t, 0) for t in offsets for s in (1, -1)] + [(0, 1), (0, -1)]
    barrier = pltpu.get_barrier_semaphore()
    expected = jnp.int32(0)
    for dx, dy in partners:

        @pl.when(exists(dx, dy))
        def _():
            pl.semaphore_signal(barrier, inc=1, device_id={"gx": gx + dx, "gy": gy + dy})

        expected = expected + exists(dx, dy).astype(jnp.int32)

    for fetch in fetches:
        fetch.wait()
    for k in range(blocks):
        for chunk in range(CHUNKS):
            piece = noisy_ref[:, chunk * rows : (chunk + 1) * rows, k * LANES : (k + 1) * LANES]
            ext[0, chunk, blocks + k] = piece.astype(jnp.float32)

    def clear_y(first):
        def step(n, _):
            zero = jnp.zeros((blocks, depth, rows, LANES), jnp.float32)
            ext[n // CHUNKS, n % CHUNKS, pl.ds(first, blocks)] = zero
            return 0

        lax.fori_loop(0, LAYERS * CHUNKS, step, 0)

    pl.when(gy == 0)(lambda: clear_y(0))
    pl.when(gy == gy_count - 1)(lambda: clear_y(2 * blocks))

    def clear_x(ref, place):
        def step(n, _):
            ref[n // depth, n % depth, pl.ds(place * width, width)] = jnp.zeros((width, LANES), jnp.float32)
            return 0

        lax.fori_loop(0, blocks * depth, step, 0)

    def place_of(i, t, sign):
        tiles = TILES[classes[i]] if modes[i] == RECEIVER else remote[i]
        slot = tiles.index(t)
        return len(tiles) - 1 - slot if sign == -1 and modes[i] == RECEIVER else slot

    for i in range(LAYERS):
        for t in remote[i]:
            pl.when(gx + t >= gx_count)(functools.partial(clear_x, above[i], place_of(i, t, 1)))
            pl.when(gx - t < 0)(functools.partial(clear_x, below[i], place_of(i, t, -1)))

    pl.semaphore_wait(barrier, expected)

    def y_copy(i, chunk, side, count=1):
        index = 0 if side == 1 else 1
        chunks = pl.ds(chunk, count)
        return pltpu.make_async_remote_copy(
            src_ref=ext.at[i, chunks, pl.ds(blocks, blocks)],
            dst_ref=ext.at[i, chunks, pl.ds(0 if side == 1 else 2 * blocks, blocks)],
            send_sem=y_send.at[i, index],
            recv_sem=y_recv.at[i, index, chunk],
            device_id={"gx": gx, "gy": gy + side},
        )

    def bases(i):
        if classes[i] == NEAR and modes[i] == RECEIVER:
            return 0, (len(TILES[NEAR]) - 1) * width
        return 0, 0

    def x_copy(i, t, sign, chunk, count=1):
        way = 0 if sign == 1 else 1
        target = (above[i], below[i])[way]
        index = remote[i].index(t) * 2 + way
        arrival = index if modes[i] == RECEIVER else index * CHUNKS + chunk
        start, size = chunk * rows, count * rows
        source = (halves[i] if is_half(i, t) else sends[i])[way]
        return pltpu.make_async_remote_copy(
            src_ref=source.at[:, :, pl.ds(bases(i)[way] + start, size)],
            dst_ref=target.at[:, :, pl.ds(place_of(i, t, sign) * width + start, size)],
            send_sem=x_send.at[sum(len(r) * 2 for r in remote[:i]) + index],
            recv_sem=x_recv.at[sum(counts[:i]) + arrival],
            device_id={"gx": gx - sign * t, "gy": gy},
        )

    def start_y(i, chunk):
        for side in (1, -1):
            pl.when(exists(0, side))(lambda: y_copy(i, chunk, side).start())

    def is_half(i, t):
        return classes[i] == HALF and t == 1

    def used(i, t, chunk):
        return (chunk < CHUNKS // 2) if is_half(i, t) else True

    def start_x(i, chunk):
        for t in SEND_ORDER[classes[i]]:
            for sign in (1, -1):
                pl.when(exists(-sign * t, 0) & used(i, t, chunk))(lambda: x_copy(i, t, sign, chunk).start())

    def wait_x(i, chunk, count=1):
        for t in SEND_ORDER[classes[i]]:
            for sign in (1, -1):
                pl.when(exists(sign * t, 0) & used(i, t, chunk))(lambda: x_copy(i, t, sign, chunk, count).wait_recv())

    lane = lax.broadcasted_iota(jnp.int32, (rows, LANES), 1)
    line = lax.broadcasted_iota(jnp.int32, (rows, LANES), 0)
    reaches = [jnp.clip(dil_ref[i], 1, blocks * LANES) for i in range(LAYERS)]

    def sums(i, chunk):
        reach = reaches[i]
        plus_tile, plus_lane = reach // LANES, reach % LANES
        minus_tile, minus_lane = (blocks * LANES - reach) // LANES, (blocks * LANES - reach) % LANES

        def shifted(tiles, choices, tile, amount):
            picked = []
            for k in range(blocks + 1):
                value = tiles[min(k + choices - 1, len(tiles) - 1)]
                for n in range(choices - 2, -1, -1):
                    value = jnp.where(tile == n, tiles[min(k + n, len(tiles) - 1)], value)
                picked.append(pltpu.roll(value, lax.rem(LANES - amount, LANES), 1))
            inside = lane < LANES - amount
            return [jnp.where(inside, picked[k], picked[k + 1]) for k in range(blocks)]

        for side in (1, -1):
            pl.when(exists(0, -side))(lambda: y_copy(i, chunk, side).wait_recv())

        def add_map(j, totals):
            totals = list(totals)
            for z_in in range(depth):
                tiles = [ext[j, chunk, n, z_in] for n in range(3 * blocks)]
                own = tiles[blocks : 2 * blocks]
                if classes[i] == FULL:
                    values = (tiles[:blocks], own, tiles[2 * blocks :])
                else:
                    values = (
                        shifted(tiles[: 2 * blocks], blocks, minus_tile, minus_lane),
                        own,
                        shifted(tiles[blocks:], blocks + 1, plus_tile, plus_lane),
                    )
                for b in range(3):
                    for z_out in range(depth):
                        c = z_in - z_out + 1
                        if c < 0 or c > 2:
                            continue
                        for a in range(3):
                            weight = w_ref[i, j, 9 * c + 3 * a + b]
                            for k in range(blocks):
                                n = (a * depth + z_out) * blocks + k
                                totals[n] = totals[n] + weight * values[b][k]
            return tuple(totals)

        totals = (jnp.zeros((rows, LANES), jnp.float32),) * (3 * depth * blocks)
        totals = lax.fori_loop(0, i + 1, add_map, totals)
        start = chunk * rows
        for z in range(depth):
            for k in range(blocks):
                up, down = totals[(2 * depth + z) * blocks + k], totals[z * blocks + k]
                if modes[i] == SENDER:
                    for half in (0, width):
                        natural[i][0][k, z, pl.ds(start + half, rows)] = up
                        natural[i][1][k, z, pl.ds(start + half, rows)] = down
                else:
                    sends[i][0][k, z, pl.ds(bases(i)[0] + start, rows)] = up
                    sends[i][1][k, z, pl.ds(bases(i)[1] + start, rows)] = down
                centre[i % 2][k, z, pl.ds(start, rows)] = totals[(depth + z) * blocks + k]
        if modes[i] != SENDER:
            start_x(i, chunk)

    def pack(i, chunk):
        turn = reaches[i] % width
        for way, first in ((0, turn), (1, width - turn)):
            for z in range(depth):
                for k in range(blocks):
                    piece = natural[i][way][k, z, pl.ds(first + chunk * rows, rows)]
                    sends[i][way][k, z, pl.ds(chunk * rows, rows)] = piece
        if classes[i] == HALF:
            low = reaches[i] < width

            @pl.when(chunk < CHUNKS // 2)
            def _():
                for way, first in ((0, turn), (1, width - turn)):
                    other = width // 2
                    skip = jnp.where(low, other, 0) if way == 0 else jnp.where(low, 0, other)
                    for z in range(depth):
                        for k in range(blocks):
                            piece = natural[i][way][k, z, pl.ds(first + skip + chunk * rows, rows)]
                            halves[i][way][k, z, pl.ds(chunk * rows, rows)] = piece

        start_x(i, chunk)

    def arrived(i, chunk):
        reach = reaches[i]
        start = chunk * rows
        if modes[i] == RECEIVER:
            least = TILES[classes[i]][0] * width
            up_start = jnp.clip(reach - least, 0, 2 * width)
            down_start = jnp.clip(2 * width + least - reach, 0, 2 * width)
            return (
                lambda k, z: above[i][k, z, pl.ds(up_start + start, rows)],
                lambda k, z: below[i][k, z, pl.ds(down_start + start, rows)],
            )
        if modes[i] == BOTH:
            return (
                lambda k, z: above[i][k, z, pl.ds(start, rows)],
                lambda k, z: below[i][k, z, pl.ds(start, rows)],
            )
        turn = reach % width
        low = reach // width == TILES[classes[i]][0]

        def choose(way, inside, k, z):
            parts = []
            for t in TILES[classes[i]]:
                if t == 0:
                    parts.append(sends[i][way][k, z, pl.ds(start, rows)])
                else:
                    place = place_of(i, t, 1) * width
                    at = lax.rem(chunk, CHUNKS // 2) * rows if is_half(i, t) else start
                    parts.append((above[i], below[i])[way][k, z, pl.ds(place + at, rows)])
            near = jnp.where(low, parts[0], parts[1])
            far = jnp.where(low, parts[1], parts[2])
            return jnp.where(inside, near, far)

        return (
            lambda k, z: choose(0, line + start + turn < width, k, z),
            lambda k, z: choose(1, line + start >= turn, k, z),
        )

    def combine(i, chunk):
        start = chunk * rows
        up, down = arrived(i, chunk)
        for z in range(depth):
            for k in range(blocks):
                value = centre[i % 2][k, z, pl.ds(start, rows)] + up(k, z) + down(k, z)
                value = jnp.maximum(value + bias_ref[i], 0.0).astype(jnp.bfloat16).astype(jnp.float32)
                if i < LAYERS - 1:
                    ext[i + 1, chunk, blocks + k, z] = value
                else:
                    mixed = mix_ref[0] * ext[0, chunk, blocks + k, z]
                    for j in range(1, LAYERS):
                        mixed = mixed + mix_ref[j] * ext[j, chunk, blocks + k, z]
                    mixed = mixed + mix_ref[LAYERS] * value
                    out_ref[z, pl.ds(start, rows), k * LANES : (k + 1) * LANES] = mixed.astype(jnp.bfloat16)
        if i < LAYERS - 1:
            start_y(i + 1, chunk)

    def loop(count, *steps):
        def step(n, _):
            for one in steps:
                one(n)
            return 0

        lax.fori_loop(0, count, step, 0)

    loop(CHUNKS, lambda chunk: start_y(0, chunk))
    for i in range(LAYERS):
        joined = i > 0 and modes[i - 1] != RECEIVER and modes[i] != SENDER
        if not joined:
            if i > 0:
                if modes[i - 1] == RECEIVER:
                    wait_x(i - 1, 0, CHUNKS)
                    loop(CHUNKS, functools.partial(combine, i - 1))
                else:
                    loop(CHUNKS, functools.partial(wait_x, i - 1), functools.partial(combine, i - 1))
            loop(CHUNKS, functools.partial(sums, i))
            if modes[i] == SENDER:
                loop(CHUNKS, functools.partial(pack, i))
        else:

            def next_sums(n):
                pl.when(n >= SKEW)(lambda: sums(i, n - SKEW))

            def last_combine(n):
                @pl.when(n < CHUNKS)
                def _():
                    wait_x(i - 1, n)
                    combine(i - 1, n)

            loop(CHUNKS + SKEW, next_sums, last_combine)
    if modes[LAYERS - 1] == RECEIVER:
        wait_x(LAYERS - 1, 0, CHUNKS)
        loop(CHUNKS, functools.partial(combine, LAYERS - 1))
    else:
        loop(CHUNKS, functools.partial(wait_x, LAYERS - 1), functools.partial(combine, LAYERS - 1))

    for i in range(LAYERS):
        for side in (1, -1):
            pl.when(exists(0, side))(lambda: y_copy(i, 0, side, CHUNKS).wait_send())
        for t in SEND_ORDER[classes[i]]:
            for sign in (1, -1):
                count = CHUNKS // 2 if is_half(i, t) else CHUNKS
                pl.when(exists(-sign * t, 0))(lambda: x_copy(i, t, sign, 0, count).wait_send())


def run(number, gx_count, gy_count, noisy, dilations, conv_weights, biases, mix_weights):
    classes = COMBOS[number]
    modes, remote, counts = plan(classes)
    depth, width, height = noisy.shape
    blocks = height // LANES
    rows = width // CHUNKS
    scratch = [pltpu.VMEM((LAYERS, CHUNKS, 3 * blocks, depth, rows, LANES), jnp.float32)]
    scratch += [pltpu.VMEM(noisy.shape, noisy.dtype)]
    scratch += [pltpu.SMEM(x.shape, x.dtype) for x in (dilations, conv_weights, biases, mix_weights)]
    scratch += [pltpu.SemaphoreType.DMA((5,))]

    def tiles(count):
        return [pltpu.VMEM((blocks, depth, count * width, LANES), jnp.float32)] * 2

    scratch += tiles(1)
    for i in range(LAYERS):
        scratch += tiles(len(TILES[classes[i]] if modes[i] == RECEIVER else remote[i]))
        if classes[i] != NEAR or modes[i] != RECEIVER:
            scratch += tiles(1)
        if modes[i] == SENDER:
            scratch += tiles(2)
        if classes[i] == HALF:
            scratch += tiles(1)
    scratch += [pltpu.SemaphoreType.DMA((LAYERS, 2)), pltpu.SemaphoreType.DMA((LAYERS, 2, CHUNKS))]
    scratch += [pltpu.SemaphoreType.DMA((sum(len(r) * 2 for r in remote),)), pltpu.SemaphoreType.DMA((sum(counts),))]
    return pl.pallas_call(
        functools.partial(kernel, classes, noisy.shape, gx_count, gy_count),
        out_shape=jax.ShapeDtypeStruct(noisy.shape, jnp.bfloat16),
        in_specs=[pl.BlockSpec(memory_space=pltpu.HBM)] * 5,
        out_specs=pl.BlockSpec(memory_space=pltpu.VMEM),
        scratch_shapes=scratch,
        compiler_params=pltpu.CompilerParams(collective_id=number, has_side_effects=True),
        name="msd_" + "".join(str(c) for c in classes),
    )(*(pltpu.with_memory_space_constraint(x, pltpu.HBM) for x in (noisy, dilations, conv_weights, biases, mix_weights)))


def body(gx_count, gy_count, noisy, dilations, conv_weights, biases, mix_weights):
    width = noisy.shape[1]
    place = lax.iota(jnp.int32, LAYERS)
    power = jnp.where(place == 0, 12, jnp.where(place == 1, 3, 1))
    small = (dilations <= width // 2) | ((dilations >= 3 * width // 2) & (dilations < 2 * width))
    kinds = (dilations >= 2 * width).astype(jnp.int32) + (dilations >= 4 * width).astype(jnp.int32)
    kinds = jnp.where(small & (place < LAYERS - 1), HALF, kinds)
    code = jnp.sum(kinds * power)
    branches = [lambda noisy, *_: jnp.zeros_like(noisy)] * 48
    for number, classes in enumerate(COMBOS):
        place = 12 * classes[0] + 3 * classes[1] + classes[2]
        branches[place] = functools.partial(run, number, gx_count, gy_count)
    return lax.switch(code, branches, noisy, dilations, conv_weights, biases, mix_weights)


def solution(mesh):
    return jax.shard_map(
        functools.partial(body, mesh.shape["gx"], mesh.shape["gy"]),
        mesh=mesh,
        in_specs=(P(None, "gx", "gy"), P(), P(), P(), P()),
        out_specs=P(None, "gx", "gy"),
        check_vma=False,
    )
```
